32 devices in a mesh: groups: 2 (over y), rows: 4 (over x, core), seq: 4 (over z).
Axes of the slice: x: 2, y: 2, z: 4, core: 2. Of those that a mesh axis runs over, the one named last changes fastest.
Arguments:
- activations: bfloat16 [2, 8, 512, 4096], P(None, ('groups', 'rows'), 'seq'), parts along dimension 1, may hold values from -6 to 6
- out_grads: bfloat16 [2, 8, 512, 4096], P(None, ('groups', 'rows'), 'seq'), parts along dimension 1, may hold values from -6 to 6
- lengths: int32 [8], P(('groups', 'rows')), parts along dimension 0, may hold values from 64 to 512
- proj_in: bfloat16 [2, 4096, 64], replicated, may hold values from -0.09375 to 0.09375
- proj_out: bfloat16 [2, 4096, 64], replicated, may hold values from -0.09375 to 0.09375
- basis_in: float32 [2, 64, 64], replicated, may hold values from -0.75 to 0.75
- basis_out: float32 [2, 64, 64], replicated, may hold values from -0.75 to 0.75
- eigen: float32 [2, 64, 64], replicated, may hold values from 10 to 1000
- store: bfloat16 [1024, 8192], P(('groups', 'rows', 'seq')), parts along dimension 0, may hold values from -0.0625 to 0.0625
- candidates: int32 [8, 64], P('groups'), parts along dimension 0, may hold values from 0 to 511
Outputs:
- scores: float32 [1024, 4], P(('groups', 'rows', 'seq')), parts along dimension 0
- picked: float32 [8, 64], P('groups'), parts along dimension 0
The draws below stay inside these ranges and needn't reach their ends.
There are 2 independent parts, one for each index of `groups`. The reference program is written for one: setup_inputs(seed, part) draws one part's arguments, and reference() takes and returns one part's arrays. A program takes and returns all parts, laid end to end along the dimension named above; an argument that names none is the same for every part. Nothing has to cross between parts.
All inputs are finite; a program needn't handle non-finite values.
Results may differ from the reference program's by a relative error of at most 0.005.
Values may be sent and summed in bfloat16 or wider, within the bound.
A program may use at most 64 MiB of HBM per device.

```python
import math
import jax
import jax.numpy as jnp
from jax import lax

D = 4096
RANK = 64
NL = 2
TOPK = 64
BATCH = 4
LENGTH = 512
ROWS_TOTAL = 512
FLAT = 8192


def draw_lengths(key, part):
    first, second = jax.random.split(jax.random.fold_in(key, 7))
    base = jax.random.randint(first, (BATCH,), LENGTH // 8, LENGTH + 1)
    chosen = jax.random.randint(second, (), 0, BATCH)
    return jnp.where(jnp.arange(BATCH) == chosen, LENGTH, base).astype(jnp.int32)


def place_ends(entries, stream_key, least, largest):
    index_at = [jax.random.randint(jax.random.fold_in(stream_key, axis), (), 0, length) for axis, length in enumerate(entries.shape)]
    longest = entries.shape.index(max(entries.shape))
    next_to = index_at[:longest] + [(index_at[longest] + 1) % entries.shape[longest]] + index_at[longest + 1:]
    return entries.at[tuple(index_at)].set(least).at[tuple(next_to)].set(largest)


def block_levels(rng, extent, cuts, least, top_value):
    loudness = 1.0
    for position, parts in cuts:
        heights = jax.random.uniform(jax.random.fold_in(jax.random.fold_in(rng, 6), position), (parts,), jnp.float32, least / len(cuts), top_value / len(cuts))
        loudness = loudness * jnp.repeat(jnp.exp(heights), extent[position] // parts).reshape((-1,) + (1,) * (len(extent) - 1 - position))
    return loudness


def gaussian(stream_key, shape, deviation, bound, shards=(), kind=jnp.bfloat16):
    array = jax.random.normal(stream_key, shape, jnp.float32) * deviation
    if len(shards) > 0:
        array = block_levels(stream_key, shape, shards, -0.22, 0.18) * array
    return jnp.clip(array, min=-bound, max=bound).astype(kind)


def setup_inputs(seed: int = 0, part: int = 0) -> dict:
    keys = jax.random.split(jax.random.key(seed), 11)
    own_keys = jax.random.split(jax.random.fold_in(keys[10], part), 11)
    activations = gaussian(own_keys[0], (NL, BATCH, LENGTH, D), 1.0, 6.0, ((1, 4), (2, 4)))
    out_grads = gaussian(own_keys[1], (NL, BATCH, LENGTH, D), 1.0, 6.0, ((1, 4), (2, 4)))
    lengths = draw_lengths(jax.random.fold_in(jax.random.fold_in(keys[10], part), 71), part)
    proj_in = gaussian(keys[3], (NL, D, RANK), D ** -0.5, 0.09375)
    proj_out = gaussian(keys[4], (NL, D, RANK), D ** -0.5, 0.09375)
    basis_in = gaussian(keys[5], (NL, RANK, RANK), RANK ** -0.5, 0.75, (), jnp.float32)
    basis_out = gaussian(keys[6], (NL, RANK, RANK), RANK ** -0.5, 0.75, (), jnp.float32)
    eigen = jnp.clip(jnp.exp(jax.random.uniform(keys[7], (NL, RANK, RANK), jnp.float32, math.log(10.0), math.log(1000.0))), 10.0, 1000.0)
    store = gaussian(own_keys[8], (ROWS_TOTAL, FLAT), FLAT ** -0.5, 0.0625, ((0, 16),))
    candidates = place_ends(jax.random.randint(own_keys[9], (BATCH, TOPK), 0, ROWS_TOTAL), jax.random.fold_in(own_keys[9], 1), 0, ROWS_TOTAL - 1).astype(jnp.int32)
    return {"activations": activations, "out_grads": out_grads, "lengths": lengths, "proj_in": proj_in, "proj_out": proj_out, "basis_in": basis_in, "basis_out": basis_out, "eigen": eigen, "store": store, "candidates": candidates}


damping = 1.0


def reference(activations, out_grads, lengths, proj_in, proj_out, basis_in, basis_out, eigen, store, candidates):
    nl, batch, length, width = activations.shape
    positions = jnp.arange(length, dtype=jnp.int32)
    mask = (positions[None, :] < lengths[:, None]).astype(jnp.bfloat16)

    def layer(items):
        acts, grads, p_in, p_out = items
        pa = jnp.dot(acts.reshape(batch * length, width), p_in, preferred_element_type=jnp.float32)
        pg = jnp.dot(grads.reshape(batch * length, width), p_out, preferred_element_type=jnp.float32)
        pa = pa.astype(jnp.bfloat16).reshape(batch, length, -1) * mask[:, :, None]
        pg = pg.astype(jnp.bfloat16).reshape(batch, length, -1) * mask[:, :, None]
        return jnp.einsum('bto,bti->boi', pg.astype(jnp.float32), pa.astype(jnp.float32), precision=lax.Precision.HIGHEST)

    grad = lax.map(layer, (activations, out_grads, proj_in, proj_out))
    high = lax.Precision.HIGHEST
    rot = jnp.einsum('loj,lboi,lik->lbjk', basis_out, grad, basis_in, precision=high)
    pre = rot / (eigen[:, None] + damping)
    back = jnp.einsum('loj,lbjk,lik->lboi', basis_out, pre, basis_in, precision=high)
    test = jnp.transpose(back, (1, 0, 2, 3)).reshape(batch, -1).astype(jnp.bfloat16)
    scores = jnp.dot(store, test.T, preferred_element_type=jnp.float32)
    picked = scores[candidates, jnp.arange(batch, dtype=jnp.int32)[:, None]]
    return scores, picked
```

```python
import functools

import jax
import jax.numpy as jnp
from jax import lax
from jax.experimental import pallas as pl
from jax.experimental.pallas import tpu as pltpu
from jax.sharding import PartitionSpec as P

damping = 1.0
MESH = pl.DeviceIdType.MESH
F32 = jnp.float32
BF16 = jnp.bfloat16
NN = (((1,), (0,)), ((), ()))
NT = (((1,), (1,)), ((), ()))
CHUNKS = 4


def mm(a, b, dims=NN):
    return lax.dot_general(a, b, dims, preferred_element_type=F32)


def split(x):
    hi = x.astype(BF16)
    return hi, (x - hi.astype(F32)).astype(BF16)


def lanes(*parts):
    return jnp.concatenate(parts, axis=1)


def stack(*parts):
    return jnp.concatenate(parts, axis=0)


def each(count, step):
    if count <= 16:
        for i in range(count):
            step(i)
    else:
        lax.fori_loop(0, count, lambda i, c: (step(i), c)[1], 0)


def kernel(
    nr, ns, nc, lengths,
    acts_hbm, grads_hbm, pin_hbm, pout_hbm, bin_hbm, bout_hbm, eig_hbm, store_hbm, cand_hbm,
    scores_ref, picked_ref,
    acts, grads, pin, pout, bin_, bout, eig, store, cand,
    tsend, trecv, total, precv, srecv, ssend,
    load_sem, small_sem, ts_sem, tr_sem, ps_sem, pr_sem, ss_sem, sr_sem, xs_sem, xr_sem,
):
    nl, tok, width = acts.shape
    rank = pin.shape[1]
    rdev = store.shape[1]
    half = rank // 2
    wide = 2 * rank
    nx = nr // nc
    n, nf = nr * ns, nx * ns
    row, seq = lax.axis_index("rows"), lax.axis_index("seq")
    mx, mc = row // nc, lax.rem(row, nc)
    me, mf = row * ns + seq, mx * ns + seq

    step = width // CHUNKS
    loads, order_ = {}, []
    for l in range(nl):
        for k in range(CHUNKS):
            at = pl.ds(k * step, step)
            for i, (src, dst) in enumerate((
                (pin_hbm.at[l, :, at], pin.at[l, :, at]),
                (acts_hbm.at[l, 0, :, at], acts.at[l, :, at]),
                (pout_hbm.at[l, :, at], pout.at[l, :, at]),
                (grads_hbm.at[l, 0, :, at], grads.at[l, :, at]),
            )):
                loads[l, k, i] = pltpu.make_async_copy(src, dst, load_sem.at[l, k, i])
                order_.append(loads[l, k, i])
    small = [
        pltpu.make_async_copy(src, dst, small_sem.at[i])
        for i, (src, dst) in enumerate((
            (bin_hbm, bin_), (bout_hbm, bout), (eig_hbm, eig), (cand_hbm, cand), (store_hbm, store.at[mc]),
        ))
    ]

    barrier = pltpu.get_barrier_semaphore()

    def peer(e):
        to = lax.rem(me + e + 1, n)
        return {"rows": to // ns, "seq": lax.rem(to, ns)}

    def friend(e):
        to = lax.rem(mf + e + 1, nf)
        return {"rows": to // ns * nc + mc, "seq": lax.rem(to, ns)}

    def sibling(e):
        return {"rows": mx * nc + lax.rem(mc + e + 1, nc)}

    each(n - 1, lambda e: pl.semaphore_signal(barrier, inc=1, device_id=peer(e), device_id_type=MESH))
    for c in small[:3]:
        c.start()
    for c in order_:
        c.start()
    for c in small[3:]:
        c.start()

    for c in small[:3]:
        c.wait()
    i0 = lax.broadcasted_iota(jnp.int32, (rank, rank), 0)
    i1 = lax.broadcasted_iota(jnp.int32, (rank, rank), 1)
    order = (i1 == jnp.where(i0 < half, 2 * i0, 2 * (i0 - half) + 1)).astype(BF16)
    w_in, w_out, w_rot, w_back, inv = [], [], [], [], []
    for l in range(nl):
        hi, lo = split(bin_[l])
        w = stack(hi, lo)
        w_in.append(lanes(w, w))
        hi, lo = split(jnp.transpose(bin_[l]))
        w = stack(hi, hi, lo, jnp.zeros_like(lo))
        w_rot.append(lanes(w, w))
        hi, lo = split(jnp.transpose(bout[l]))
        w_out.append(lanes(hi, lo))
        hi, lo = (mm(order, x).astype(BF16) for x in split(bout[l]))
        w_back.append(lanes(hi, hi, lo))
        v = 1.0 / (eig[l] + damping)
        inv.append(lanes(v, v))

    pos = seq * tok + lax.broadcasted_iota(jnp.int32, (tok, rank), 0)
    keep = pos < lengths[0]
    low = lax.broadcasted_iota(jnp.int32, (rank, wide), 1) < rank
    for l in range(nl):
        pa = pgt = None
        for k in range(CHUNKS):
            at = slice(k * step, (k + 1) * step)
            loads[l, k, 0].wait()
            loads[l, k, 1].wait()
            a = mm(acts[l, :, at], pin[l, :, at], NT)
            pa = a if k == 0 else pa + a
            loads[l, k, 2].wait()
            loads[l, k, 3].wait()
            a = mm(pout[l, :, at], grads[l, :, at], NT)
            pgt = a if k == 0 else pgt + a
        pa = jnp.where(keep, pa.astype(BF16).astype(F32), 0.0).astype(BF16)
        pgt = pgt.astype(BF16)
        u_hi, u_lo = split(mm(lanes(pa, pa), w_in[l]))
        v_hi, v_lo = split(mm(w_out[l], stack(pgt, pgt)))
        rot = mm(lanes(v_hi, v_lo, v_hi), stack(u_hi, u_hi, u_lo))
        hi, lo = split(rot * inv[l])
        x2 = mm(lanes(jnp.where(low, hi, lo), hi), w_rot[l])
        hi, lo = split(x2)
        z = mm(w_back[l], stack(hi, lo, hi))
        tsend[pl.ds(l * half, half), :] = jnp.where(low[:half], z[:half], z[half:]).astype(BF16)

    pl.semaphore_wait(barrier, n - 1)

    def tcopy(e):
        return pltpu.make_async_remote_copy(
            src_ref=tsend, dst_ref=trecv.at[mf], send_sem=ts_sem.at[0], recv_sem=tr_sem.at[0],
            device_id=friend(e), device_id_type=MESH)

    def xcopy(e):
        return pltpu.make_async_remote_copy(
            src_ref=store.at[mc], dst_ref=store.at[mc], send_sem=xs_sem.at[e], recv_sem=xr_sem.at[e],
            device_id=sibling(e), device_id_type=MESH)

    each(nf - 1, lambda e: tcopy(e).start())
    for c in small[3:]:
        c.wait()
    each(nc - 1, lambda e: xcopy(e).start())
    trecv[pl.ds(mf, 1)] = tsend[...][None]

    rows = nc * rdev
    eye = lax.broadcasted_iota(jnp.int32, (rows, rdev), 0)
    col_of = lax.broadcasted_iota(jnp.int32, (rows, rdev), 1)
    r = lax.broadcasted_iota(jnp.int32, (rows, cand.shape[1]), 0)
    rows_k = ((mx * nc + r // rdev) * ns + seq) * rdev + lax.rem(r, rdev)

    each(nc - 1, lambda e: xcopy(e).wait_recv())
    others = trecv.at[pl.ds(0, nf - 1)]
    pltpu.make_async_copy(others, others, tr_sem.at[0]).wait()
    for x in range(nx):
        t = trecv[x * ns].astype(F32)
        for s in range(1, ns):
            t = t + trecv[x * ns + s].astype(F32)
        total[x] = t
    acc = [jnp.zeros((rows, wide), F32) for _ in range(nx)]
    for c in range(nl * half):
        s = store[:, :, c * wide:(c + 1) * wide].astype(F32).reshape(rows, wide)
        for x in range(nx):
            acc[x] = acc[x] + s * total[x, c:c + 1, :]
    cols = [jnp.sum(a, axis=1, keepdims=True) for a in acc]
    for x in range(nx):
        hit = cand[pl.ds(x * nc + mc, 1), :] == rows_k
        precv[pl.ds(me, 1), x:x + 1, :] = jnp.sum(jnp.where(hit, cols[x], 0.0), axis=0, keepdims=True)[None]

    def pcopy(e):
        return pltpu.make_async_remote_copy(
            src_ref=precv.at[me], dst_ref=precv.at[me], send_sem=ps_sem.at[0], recv_sem=pr_sem.at[0],
            device_id=peer(e), device_id_type=MESH)

    each(n - 1, lambda e: pcopy(e).start())

    for x in range(nx):
        for c in range(nc):
            ssend[c, x:x + 1, :] = jnp.sum(
                jnp.where(eye == col_of + c * rdev, cols[x], 0.0), axis=0, keepdims=True)

    def scopy(e):
        return pltpu.make_async_remote_copy(
            src_ref=ssend.at[lax.rem(mc + e + 1, nc)], dst_ref=srecv.at[mc],
            send_sem=ss_sem.at[e], recv_sem=sr_sem.at[e],
            device_id=sibling(e), device_id_type=MESH)

    each(nc - 1, lambda e: scopy(e).start())
    srecv[pl.ds(mc, 1)] = ssend[pl.ds(mc, 1)]
    each(nc - 1, lambda e: scopy(e).wait_recv())
    for x in range(nx):
        for c in range(nc):
            scores_ref[x * nc + c:x * nc + c + 1, :] = srecv[c, x:x + 1, :]
    each(nc - 1, lambda e: scopy(e).wait_send())
    each(nc - 1, lambda e: xcopy(e).wait_send())
    pltpu.make_async_copy(others, others, ts_sem.at[0]).wait()

    others = precv.at[pl.ds(0, n - 1)]
    pltpu.make_async_copy(others, others, pr_sem.at[0]).wait()
    for c in range(nc):
        p = None
        for x in range(nx):
            at = (x * nc + c) * ns
            q = jnp.sum(precv[at:at + ns], axis=0)
            p = q if p is None else p + q
        for x in range(nx):
            picked_ref[x * nc + c:x * nc + c + 1, :] = p[x:x + 1, :]
    pltpu.make_async_copy(others, others, ps_sem.at[0]).wait()


def body(nr, ns, activations, out_grads, lengths, proj_in, proj_out,
         basis_in, basis_out, eigen, store, candidates):
    nl, _, tok, width = activations.shape
    rank = proj_in.shape[2]
    rdev, flat = store.shape
    batch, topk = candidates.shape
    nc = 2 if nr % 2 == 0 else 1
    nx = nr // nc
    n, nf = nr * ns, nx * ns
    dma = pltpu.SemaphoreType.DMA
    vm = pltpu.VMEM
    hbm = pl.BlockSpec(memory_space=pltpu.HBM)
    scores, picked = pl.pallas_call(
        functools.partial(kernel, nr, ns, nc),
        out_shape=(pltpu.VMEM((batch, rdev), F32), pltpu.VMEM((batch, topk), F32)),
        in_specs=[pl.BlockSpec(memory_space=pltpu.SMEM)] + [hbm] * 9,
        out_specs=(pl.BlockSpec(memory_space=pltpu.VMEM),) * 2,
        scratch_shapes=[
            vm((nl, tok, width), BF16), vm((nl, tok, width), BF16),
            vm((nl, rank, width), BF16), vm((nl, rank, width), BF16),
            vm((nl, rank, rank), F32), vm((nl, rank, rank), F32), vm((nl, rank, rank), F32),
            vm((nc, rdev, flat), BF16), vm((batch, topk), jnp.int32),
            vm((nl * rank // 2, 2 * rank), BF16), vm((nf, nl * rank // 2, 2 * rank), BF16),
            vm((nx, nl * rank // 2, 2 * rank), F32),
            vm((n, nx, topk), F32), vm((nc, nx, rdev), F32), vm((nc, nx, rdev), F32),
            dma((nl, CHUNKS, 4)), dma((5,)),
            dma((1,)), dma((1,)), dma((1,)), dma((1,)),
            dma((nc,)), dma((nc,)), dma((nc,)), dma((nc,)),
        ],
        compiler_params=pltpu.CompilerParams(
            collective_id=0, has_side_effects=True, vmem_limit_bytes=60 * 2**20),
    )(
        lengths, activations, out_grads,
        jnp.swapaxes(proj_in, 1, 2), jnp.swapaxes(proj_out, 1, 2),
        basis_in, basis_out, eigen, store, candidates,
    )
    return scores.T, picked


def solution(mesh):
    placed = (
        P(None, ("groups", "rows"), "seq", None),
        P(None, ("groups", "rows"), "seq", None),
        P(("groups", "rows")),
        P(),
        P(),
        P(),
        P(),
        P(),
        P(("groups", "rows", "seq"), None),
        P("groups", None),
    )
    return jax.shard_map(
        functools.partial(body, mesh.shape["rows"], mesh.shape["seq"]),
        mesh=mesh,
        in_specs=placed,
        out_specs=(P(("groups", "rows", "seq"), None), P("groups", None)),
        check_vma=False,
    )
```

```python
import functools

import jax
import jax.numpy as jnp
from jax import lax
from jax.experimental import pallas as pl
from jax.experimental.pallas import tpu as pltpu
from jax.sharding import PartitionSpec as P

damping = 1.0
MESH = pl.DeviceIdType.MESH
F32 = jnp.float32
BF16 = jnp.bfloat16
NN = (((1,), (0,)), ((), ()))
NT = (((1,), (1,)), ((), ()))


def mm(a, b, dims=NN):
    return lax.dot_general(a, b, dims, preferred_element_type=F32)


def split(x):
    hi = x.astype(BF16)
    return hi, (x - hi.astype(F32)).astype(BF16)


def lanes(*parts):
    return jnp.concatenate(parts, axis=1)


def stack(*parts):
    return jnp.concatenate(parts, axis=0)


def each(count, step):
    if count <= 16:
        for i in range(count):
            step(i)
    else:
        lax.fori_loop(0, count, lambda i, c: (step(i), c)[1], 0)


def kernel(
    nr, ns, nc, lengths,
    acts_hbm, grads_hbm, pin_hbm, pout_hbm, bin_hbm, bout_hbm, eig_hbm, store_hbm, cand_hbm,
    scores_ref, picked_ref,
    acts, grads, pin, pout, bin_, bout, eig, store, cand,
    tsend, trecv, total, precv, srecv, ssend,
    load_sem, small_sem, ts_sem, tr_sem, ps_sem, pr_sem, ss_sem, sr_sem, xs_sem, xr_sem,
):
    nl, tok, width = acts.shape
    rank = pin.shape[1]
    rdev = store.shape[1]
    half = rank // 2
    wide = 2 * rank
    nx = nr // nc
    n, nf = nr * ns, nx * ns
    row, seq = lax.axis_index("rows"), lax.axis_index("seq")
    mx, mc = row // nc, lax.rem(row, nc)
    me, mf = row * ns + seq, mx * ns + seq

    groups = []
    for l in range(nl):
        copies = (
            (pin_hbm.at[l], pin.at[l]), (pout_hbm.at[l], pout.at[l]),
            (acts_hbm.at[l, 0], acts.at[l]), (grads_hbm.at[l, 0], grads.at[l]),
        )
        groups.append([pltpu.make_async_copy(src, dst, load_sem.at[l, i]) for i, (src, dst) in enumerate(copies)])
    small = [
        pltpu.make_async_copy(src, dst, small_sem.at[i])
        for i, (src, dst) in enumerate((
            (bin_hbm, bin_), (bout_hbm, bout), (eig_hbm, eig), (cand_hbm, cand), (store_hbm, store.at[mc]),
        ))
    ]

    barrier = pltpu.get_barrier_semaphore()

    def peer(e):
        to = lax.rem(me + e + 1, n)
        return {"rows": to // ns, "seq": lax.rem(to, ns)}

    def friend(e):
        to = lax.rem(mf + e + 1, nf)
        return {"rows": to // ns * nc + mc, "seq": lax.rem(to, ns)}

    def sibling(e):
        return {"rows": mx * nc + lax.rem(mc + e + 1, nc)}

    for c in small[:3]:
        c.start()
    for g in groups:
        for c in g:
            c.start()
    for c in small[3:]:
        c.start()

    each(n - 1, lambda e: pl.semaphore_signal(barrier, inc=1, device_id=peer(e), device_id_type=MESH))
    for c in small[:3]:
        c.wait()
    i0 = lax.broadcasted_iota(jnp.int32, (rank, rank), 0)
    i1 = lax.broadcasted_iota(jnp.int32, (rank, rank), 1)
    order = (i1 == jnp.where(i0 < half, 2 * i0, 2 * (i0 - half) + 1)).astype(BF16)
    w_in, w_out, w_rot, w_back, inv = [], [], [], [], []
    for l in range(nl):
        hi, lo = split(bin_[l])
        w = stack(hi, lo)
        w_in.append(lanes(w, w))
        hi, lo = split(jnp.transpose(bin_[l]))
        w = stack(hi, hi, lo, jnp.zeros_like(lo))
        w_rot.append(lanes(w, w))
        hi, lo = split(jnp.transpose(bout[l]))
        w_out.append(lanes(hi, lo))
        hi, lo = (mm(order, x).astype(BF16) for x in split(bout[l]))
        w_back.append(lanes(hi, hi, lo))
        v = 1.0 / (eig[l] + damping)
        inv.append(lanes(v, v))

    pos = seq * tok + lax.broadcasted_iota(jnp.int32, (tok, rank), 0)
    keep = pos < lengths[0]
    low = lax.broadcasted_iota(jnp.int32, (rank, wide), 1) < rank
    pa, pgt = [None] * nl, [None] * nl
    for l in range(nl):
        for c in groups[l]:
            c.wait()
        pa[l] = mm(acts[l], pin[l], NT)
        pgt[l] = mm(pout[l], grads[l], NT)
    ls = range(nl)
    pa = [jnp.where(keep, x.astype(BF16).astype(F32), 0.0).astype(BF16) for x in pa]
    pgt = [x.astype(BF16) for x in pgt]
    u = [split(mm(lanes(pa[l], pa[l]), w_in[l])) for l in ls]
    v = [split(mm(w_out[l], stack(pgt[l], pgt[l]))) for l in ls]
    rot = [mm(lanes(v[l][0], v[l][1], v[l][0]), stack(u[l][0], u[l][0], u[l][1])) for l in ls]
    pre = [split(rot[l] * inv[l]) for l in ls]
    x2 = [split(mm(lanes(jnp.where(low, *pre[l]), pre[l][0]), w_rot[l])) for l in ls]
    z = [mm(w_back[l], stack(x2[l][0], x2[l][1], x2[l][0])) for l in ls]
    for l in ls:
        tsend[pl.ds(l * half, half), :] = jnp.where(low[:half], z[l][:half], z[l][half:]).astype(BF16)

    pl.semaphore_wait(barrier, n - 1)

    def tcopy(e):
        return pltpu.make_async_remote_copy(
            src_ref=tsend, dst_ref=trecv.at[mf], send_sem=ts_sem.at[0], recv_sem=tr_sem.at[0],
            device_id=friend(e), device_id_type=MESH)

    def xcopy(e):
        return pltpu.make_async_remote_copy(
            src_ref=store.at[mc], dst_ref=store.at[mc], send_sem=xs_sem.at[e], recv_sem=xr_sem.at[e],
            device_id=sibling(e), device_id_type=MESH)

    each(nf - 1, lambda e: tcopy(e).start())
    for c in small[3:]:
        c.wait()
    each(nc - 1, lambda e: xcopy(e).start())
    trecv[pl.ds(mf, 1)] = tsend[...][None]

    rows = nc * rdev
    eye = lax.broadcasted_iota(jnp.int32, (rows, rdev), 0)
    col_of = lax.broadcasted_iota(jnp.int32, (rows, rdev), 1)
    r = lax.broadcasted_iota(jnp.int32, (rows, cand.shape[1]), 0)
    rows_k = ((mx * nc + r // rdev) * ns + seq) * rdev + lax.rem(r, rdev)

    each(nc - 1, lambda e: xcopy(e).wait_recv())
    others = trecv.at[pl.ds(0, nf - 1)]
    pltpu.make_async_copy(others, others, tr_sem.at[0]).wait()
    for x in range(nx):
        t = trecv[x * ns].astype(F32)
        for s in range(1, ns):
            t = t + trecv[x * ns + s].astype(F32)
        total[x] = t
    acc = [jnp.zeros((rows, wide), F32) for _ in range(nx)]
    for c in range(nl * half):
        s = store[:, :, c * wide:(c + 1) * wide].astype(F32).reshape(rows, wide)
        for x in range(nx):
            acc[x] = acc[x] + s * total[x, c:c + 1, :]
    cols = [jnp.sum(a, axis=1, keepdims=True) for a in acc]
    for x in range(nx):
        hit = cand[pl.ds(x * nc + mc, 1), :] == rows_k
        precv[pl.ds(me, 1), x:x + 1, :] = jnp.sum(jnp.where(hit, cols[x], 0.0), axis=0, keepdims=True)[None]

    def pcopy(e):
        return pltpu.make_async_remote_copy(
            src_ref=precv.at[me], dst_ref=precv.at[me], send_sem=ps_sem.at[0], recv_sem=pr_sem.at[0],
            device_id=peer(e), device_id_type=MESH)

    each(n - 1, lambda e: pcopy(e).start())

    for x in range(nx):
        for c in range(nc):
            ssend[c, x:x + 1, :] = jnp.sum(
                jnp.where(eye == col_of + c * rdev, cols[x], 0.0), axis=0, keepdims=True)

    def scopy(e):
        return pltpu.make_async_remote_copy(
            src_ref=ssend.at[lax.rem(mc + e + 1, nc)], dst_ref=srecv.at[mc],
            send_sem=ss_sem.at[e], recv_sem=sr_sem.at[e],
            device_id=sibling(e), device_id_type=MESH)

    each(nc - 1, lambda e: scopy(e).start())
    srecv[pl.ds(mc, 1)] = ssend[pl.ds(mc, 1)]
    each(nc - 1, lambda e: scopy(e).wait_recv())
    for x in range(nx):
        for c in range(nc):
            scores_ref[x * nc + c:x * nc + c + 1, :] = srecv[c, x:x + 1, :]
    each(nc - 1, lambda e: scopy(e).wait_send())
    each(nc - 1, lambda e: xcopy(e).wait_send())
    pltpu.make_async_copy(others, others, ts_sem.at[0]).wait()

    others = precv.at[pl.ds(0, n - 1)]
    pltpu.make_async_copy(others, others, pr_sem.at[0]).wait()
    for c in range(nc):
        p = None
        for x in range(nx):
            at = (x * nc + c) * ns
            q = jnp.sum(precv[at:at + ns], axis=0)
            p = q if p is None else p + q
        for x in range(nx):
            picked_ref[x * nc + c:x * nc + c + 1, :] = p[x:x + 1, :]
    pltpu.make_async_copy(others, others, ps_sem.at[0]).wait()


def body(nr, ns, activations, out_grads, lengths, proj_in, proj_out,
         basis_in, basis_out, eigen, store, candidates):
    nl, _, tok, width = activations.shape
    rank = proj_in.shape[2]
    rdev, flat = store.shape
    batch, topk = candidates.shape
    nc = 2 if nr % 2 == 0 else 1
    nx = nr // nc
    n, nf = nr * ns, nx * ns
    dma = pltpu.SemaphoreType.DMA
    vm = pltpu.VMEM
    hbm = pl.BlockSpec(memory_space=pltpu.HBM)
    scores, picked = pl.pallas_call(
        functools.partial(kernel, nr, ns, nc),
        out_shape=(pltpu.VMEM((batch, rdev), F32), pltpu.VMEM((batch, topk), F32)),
        in_specs=[pl.BlockSpec(memory_space=pltpu.SMEM)] + [hbm] * 9,
        out_specs=(pl.BlockSpec(memory_space=pltpu.VMEM),) * 2,
        scratch_shapes=[
            vm((nl, tok, width), BF16), vm((nl, tok, width), BF16),
            vm((nl, rank, width), BF16), vm((nl, rank, width), BF16),
            vm((nl, rank, rank), F32), vm((nl, rank, rank), F32), vm((nl, rank, rank), F32),
            vm((nc, rdev, flat), BF16), vm((batch, topk), jnp.int32),
            vm((nl * rank // 2, 2 * rank), BF16), vm((nf, nl * rank // 2, 2 * rank), BF16),
            vm((nx, nl * rank // 2, 2 * rank), F32),
            vm((n, nx, topk), F32), vm((nc, nx, rdev), F32), vm((nc, nx, rdev), F32),
            dma((nl, 4)), dma((5,)),
            dma((1,)), dma((1,)), dma((1,)), dma((1,)),
            dma((nc,)), dma((nc,)), dma((nc,)), dma((nc,)),
        ],
        compiler_params=pltpu.CompilerParams(
            collective_id=0, has_side_effects=True, vmem_limit_bytes=60 * 2**20),
    )(
        lengths, activations, out_grads,
        jnp.swapaxes(proj_in, 1, 2), jnp.swapaxes(proj_out, 1, 2),
        basis_in, basis_out, eigen, store, candidates,
    )
    return scores.T, picked


def solution(mesh):
    placed = (
        P(None, ("groups", "rows"), "seq", None),
        P(None, ("groups", "rows"), "seq", None),
        P(("groups", "rows")),
        P(),
        P(),
        P(),
        P(),
        P(),
        P(("groups", "rows", "seq"), None),
        P("groups", None),
    )
    return jax.shard_map(
        functools.partial(body, mesh.shape["rows"], mesh.shape["seq"]),
        mesh=mesh,
        in_specs=placed,
        out_specs=(P(("groups", "rows", "seq"), None), P("groups", None)),
        check_vma=False,
    )
```

```python
import functools

import jax
import jax.numpy as jnp
from jax import lax
from jax.experimental import pallas as pl
from jax.experimental.pallas import tpu as pltpu
from jax.sharding import PartitionSpec as P

damping = 1.0
MESH = pl.DeviceIdType.MESH
F32 = jnp.float32
BF16 = jnp.bfloat16
NN = (((1,), (0,)), ((), ()))
NT = (((1,), (1,)), ((), ()))


def mm(a, b, dims=NN):
    return lax.dot_general(a, b, dims, preferred_element_type=F32)


def split(x):
    hi = x.astype(BF16)
    return hi, (x - hi.astype(F32)).astype(BF16)


def lanes(*parts):
    return jnp.concatenate(parts, axis=1)


def stack(*parts):
    return jnp.concatenate(parts, axis=0)


def flip(i, size, mask):
    out, bit = 0, 1
    while bit < size:
        b = lax.rem(i // bit, 2)
        out = out + bit * (1 - b if mask & bit else b)
        bit *= 2
    return out


def each(count, step):
    if count <= 16:
        for i in range(count):
            step(i)
    else:
        lax.fori_loop(0, count, lambda i, c: (step(i), c)[1], 0)


def kernel(
    nr, ns, nc, lengths,
    acts_hbm, grads_hbm, pin_hbm, pout_hbm, bin_hbm, bout_hbm, eig_hbm, store_hbm, cand_hbm,
    scores_ref, picked_ref,
    acts, grads, pin, pout, bin_, bout, eig, store, cand,
    storef, tsend, trecv, total, precv, srecv, ssend,
    load_sem, small_sem, ts_sem, tr_sem, ps_sem, pr_sem, ss_sem, sr_sem, xs_sem, xr_sem,
):
    nl, tok, width = acts.shape
    rank = pin.shape[1]
    rdev = store.shape[1]
    half = rank // 2
    wide = 2 * rank
    nx = nr // nc
    n, nf = nr * ns, nx * ns
    row, seq = lax.axis_index("rows"), lax.axis_index("seq")
    mx, mc = row // nc, lax.rem(row, nc)
    me, mf = row * ns + seq, mx * ns + seq

    groups = []
    for l in range(nl):
        copies = (
            (pin_hbm.at[l], pin.at[l]), (pout_hbm.at[l], pout.at[l]),
            (acts_hbm.at[l, 0], acts.at[l]), (grads_hbm.at[l, 0], grads.at[l]),
        )
        groups.append([pltpu.make_async_copy(src, dst, load_sem.at[l, i]) for i, (src, dst) in enumerate(copies)])
    small = [
        pltpu.make_async_copy(src, dst, small_sem.at[i])
        for i, (src, dst) in enumerate((
            (bin_hbm, bin_), (bout_hbm, bout), (eig_hbm, eig), (cand_hbm, cand), (store_hbm, store.at[mc]),
        ))
    ]

    barrier = pltpu.get_barrier_semaphore()

    far = n <= 16 and n & (n - 1) == 0
    masks = [(x, z, c) for z in reversed(range(ns)) for x in reversed(range(nx)) for c in range(nc)]

    def peer(e):
        if far:
            x, z, c = [m for m in masks if any(m)][e]
            return {"rows": flip(mx, nx, x) * nc + flip(mc, nc, c), "seq": flip(seq, ns, z)}
        to = lax.rem(me + e + 1, n)
        return {"rows": to // ns, "seq": lax.rem(to, ns)}

    def friend(e):
        if far:
            x, z, _ = [m for m in masks if any(m[:2]) and m[2] == 0][e]
            return {"rows": flip(mx, nx, x) * nc + mc, "seq": flip(seq, ns, z)}
        to = lax.rem(mf + e + 1, nf)
        return {"rows": to // ns * nc + mc, "seq": lax.rem(to, ns)}

    def sibling(e):
        return {"rows": mx * nc + lax.rem(mc + e + 1, nc)}

    for c in small[:3]:
        c.start()
    for c in groups[0]:
        c.start()
    each(n - 1, lambda e: pl.semaphore_signal(barrier, inc=1, device_id=peer(e), device_id_type=MESH))
    for g in groups[1:]:
        for c in g:
            c.start()
    for c in small[3:]:
        c.start()
    for c in small[:3]:
        c.wait()
    i0 = lax.broadcasted_iota(jnp.int32, (rank, rank), 0)
    i1 = lax.broadcasted_iota(jnp.int32, (rank, rank), 1)
    order = (i1 == jnp.where(i0 < half, 2 * i0, 2 * (i0 - half) + 1)).astype(BF16)
    w_in, w_out, w_rot, w_back, inv = [], [], [], [], []
    for l in range(nl):
        hi, lo = split(bin_[l])
        w = stack(hi, lo)
        w_in.append(lanes(w, w))
        hi, lo = split(jnp.transpose(bin_[l]))
        w = stack(hi, hi, lo, jnp.zeros_like(lo))
        w_rot.append(lanes(w, w))
        hi, lo = split(jnp.transpose(bout[l]))
        w_out.append(lanes(hi, lo))
        hi, lo = (mm(order, x).astype(BF16) for x in split(bout[l]))
        w_back.append(lanes(hi, hi, lo))
        v = 1.0 / (eig[l] + damping)
        inv.append(lanes(v, v))

    pos = seq * tok + lax.broadcasted_iota(jnp.int32, (tok, rank), 0)
    keep = pos < lengths[0]
    low = lax.broadcasted_iota(jnp.int32, (rank, wide), 1) < rank
    pa, pgt = [None] * nl, [None] * nl
    for l in range(nl):
        for c in groups[l]:
            c.wait()
        pa[l] = mm(acts[l], pin[l], NT)
        pgt[l] = mm(pout[l], grads[l], NT)
    ls = range(nl)
    pa = [jnp.where(keep, x.astype(BF16).astype(F32), 0.0).astype(BF16) for x in pa]
    pgt = [x.astype(BF16) for x in pgt]
    u = [split(mm(lanes(pa[l], pa[l]), w_in[l])) for l in ls]
    v = [split(mm(w_out[l], stack(pgt[l], pgt[l]))) for l in ls]
    rot = [mm(lanes(v[l][0], v[l][1], v[l][0]), stack(u[l][0], u[l][0], u[l][1])) for l in ls]
    pre = [split(rot[l] * inv[l]) for l in ls]
    x2 = [split(mm(lanes(jnp.where(low, *pre[l]), pre[l][0]), w_rot[l])) for l in ls]
    z = [mm(w_back[l], stack(x2[l][0], x2[l][1], x2[l][0])) for l in ls]
    for l in ls:
        tsend[pl.ds(l * half, half), :] = jnp.where(low[:half], z[l][:half], z[l][half:]).astype(BF16)

    pl.semaphore_wait(barrier, n - 1)

    def tcopy(e):
        return pltpu.make_async_remote_copy(
            src_ref=tsend, dst_ref=trecv.at[mf], send_sem=ts_sem.at[0], recv_sem=tr_sem.at[0],
            device_id=friend(e), device_id_type=MESH)

    def xcopy(e):
        return pltpu.make_async_remote_copy(
            src_ref=store.at[mc], dst_ref=store.at[mc], send_sem=xs_sem.at[e], recv_sem=xr_sem.at[e],
            device_id=sibling(e), device_id_type=MESH)

    each(nf - 1, lambda e: tcopy(e).start())
    for c in small[3:]:
        c.wait()
    each(nc - 1, lambda e: xcopy(e).start())
    trecv[pl.ds(mf, 1)] = tsend[...][None]

    rows = nc * rdev
    eye = lax.broadcasted_iota(jnp.int32, (rows, rdev), 0)
    col_of = lax.broadcasted_iota(jnp.int32, (rows, rdev), 1)
    r = lax.broadcasted_iota(jnp.int32, (rows, cand.shape[1]), 0)
    rows_k = ((mx * nc + r // rdev) * ns + seq) * rdev + lax.rem(r, rdev)

    hits = [cand[pl.ds(x * nc + mc, 1), :] == rows_k for x in range(nx)]
    each(nc - 1, lambda e: xcopy(e).wait_recv())
    for c in range(nl * half):
        at = slice(c * wide, (c + 1) * wide)
        storef[:, at] = store[:, :, at].astype(F32).reshape(rows, wide)
    others = trecv.at[pl.ds(0, nf - 1)]
    pltpu.make_async_copy(others, others, tr_sem.at[0]).wait()
    for x in range(nx):
        t = trecv[x * ns].astype(F32)
        for s in range(1, ns):
            t = t + trecv[x * ns + s].astype(F32)
        total[x] = t
    acc = [jnp.zeros((rows, wide), F32) for _ in range(nx)]
    for c in range(nl * half):
        s = storef[:, c * wide:(c + 1) * wide]
        for x in range(nx):
            acc[x] = acc[x] + s * total[x, c:c + 1, :]
    cols = [jnp.sum(a, axis=1, keepdims=True) for a in acc]
    for x in range(nx):
        precv[pl.ds(me, 1), x:x + 1, :] = jnp.sum(jnp.where(hits[x], cols[x], 0.0), axis=0, keepdims=True)[None]

    def pcopy(e):
        return pltpu.make_async_remote_copy(
            src_ref=precv.at[me], dst_ref=precv.at[me], send_sem=ps_sem.at[0], recv_sem=pr_sem.at[0],
            device_id=peer(e), device_id_type=MESH)

    each(n - 1, lambda e: pcopy(e).start())

    for x in range(nx):
        for c in range(nc):
            ssend[c, x:x + 1, :] = jnp.sum(
                jnp.where(eye == col_of + c * rdev, cols[x], 0.0), axis=0, keepdims=True)

    def scopy(e):
        return pltpu.make_async_remote_copy(
            src_ref=ssend.at[lax.rem(mc + e + 1, nc)], dst_ref=srecv.at[mc],
            send_sem=ss_sem.at[e], recv_sem=sr_sem.at[e],
            device_id=sibling(e), device_id_type=MESH)

    each(nc - 1, lambda e: scopy(e).start())
    srecv[pl.ds(mc, 1)] = ssend[pl.ds(mc, 1)]
    each(nc - 1, lambda e: scopy(e).wait_recv())
    for x in range(nx):
        for c in range(nc):
            scores_ref[x * nc + c:x * nc + c + 1, :] = srecv[c, x:x + 1, :]
    each(nc - 1, lambda e: scopy(e).wait_send())
    each(nc - 1, lambda e: xcopy(e).wait_send())
    pltpu.make_async_copy(others, others, ts_sem.at[0]).wait()

    others = precv.at[pl.ds(0, n - 1)]
    pltpu.make_async_copy(others, others, pr_sem.at[0]).wait()
    for c in range(nc):
        p = None
        for x in range(nx):
            at = (x * nc + c) * ns
            q = jnp.sum(precv[at:at + ns], axis=0)
            p = q if p is None else p + q
        for x in range(nx):
            picked_ref[x * nc + c:x * nc + c + 1, :] = p[x:x + 1, :]
    pltpu.make_async_copy(others, others, ps_sem.at[0]).wait()


def body(nr, ns, activations, out_grads, lengths, proj_in, proj_out,
         basis_in, basis_out, eigen, store, candidates):
    nl, _, tok, width = activations.shape
    rank = proj_in.shape[2]
    rdev, flat = store.shape
    batch, topk = candidates.shape
    nc = 2 if nr % 2 == 0 else 1
    nx = nr // nc
    n, nf = nr * ns, nx * ns
    dma = pltpu.SemaphoreType.DMA
    vm = pltpu.VMEM
    hbm = pl.BlockSpec(memory_space=pltpu.HBM)
    scores, picked = pl.pallas_call(
        functools.partial(kernel, nr, ns, nc),
        out_shape=(pltpu.VMEM((batch, rdev), F32), pltpu.VMEM((batch, topk), F32)),
        in_specs=[pl.BlockSpec(memory_space=pltpu.SMEM)] + [hbm] * 9,
        out_specs=(pl.BlockSpec(memory_space=pltpu.VMEM),) * 2,
        scratch_shapes=[
            vm((nl, tok, width), BF16), vm((nl, tok, width), BF16),
            vm((nl, rank, width), BF16), vm((nl, rank, width), BF16),
            vm((nl, rank, rank), F32), vm((nl, rank, rank), F32), vm((nl, rank, rank), F32),
            vm((nc, rdev, flat), BF16), vm((batch, topk), jnp.int32),
            vm((nc * rdev, flat), F32),
            vm((nl * rank // 2, 2 * rank), BF16), vm((nf, nl * rank // 2, 2 * rank), BF16),
            vm((nx, nl * rank // 2, 2 * rank), F32),
            vm((n, nx, topk), F32), vm((nc, nx, rdev), F32), vm((nc, nx, rdev), F32),
            dma((nl, 4)), dma((5,)),
            dma((1,)), dma((1,)), dma((1,)), dma((1,)),
            dma((nc,)), dma((nc,)), dma((nc,)), dma((nc,)),
        ],
        compiler_params=pltpu.CompilerParams(
            collective_id=0, has_side_effects=True, vmem_limit_bytes=60 * 2**20),
    )(
        lengths, activations, out_grads,
        jnp.swapaxes(proj_in, 1, 2), jnp.swapaxes(proj_out, 1, 2),
        basis_in, basis_out, eigen, store, candidates,
    )
    return scores.T, picked


def solution(mesh):
    placed = (
        P(None, ("groups", "rows"), "seq", None),
        P(None, ("groups", "rows"), "seq", None),
        P(("groups", "rows")),
        P(),
        P(),
        P(),
        P(),
        P(),
        P(("groups", "rows", "seq"), None),
        P("groups", None),
    )
    return jax.shard_map(
        functools.partial(body, mesh.shape["rows"], mesh.shape["seq"]),
        mesh=mesh,
        in_specs=placed,
        out_specs=(P(("groups", "rows", "seq"), None), P("groups", None)),
        check_vma=False,
    )
```

```python
import functools

import jax
import jax.numpy as jnp
from jax import lax
from jax.experimental import pallas as pl
from jax.experimental.pallas import tpu as pltpu
from jax.sharding import PartitionSpec as P

damping = 1.0
MESH = pl.DeviceIdType.MESH
F32 = jnp.float32
BF16 = jnp.bfloat16
NN = (((1,), (0,)), ((), ()))
NT = (((1,), (1,)), ((), ()))


def mm(a, b, dims=NN):
    return lax.dot_general(a, b, dims, preferred_element_type=F32)


def split(x):
    hi = x.astype(BF16)
    return hi, (x - hi.astype(F32)).astype(BF16)


def lanes(*parts):
    return jnp.concatenate(parts, axis=1)


def stack(*parts):
    return jnp.concatenate(parts, axis=0)


def farther(i, size, k):
    end = 2 * i // size
    near = i + end * (size - 1 - 2 * i)
    at = size - 1 - k
    at = at - (near - at + size) // size
    return at + end * (size - 1 - 2 * at)


def each(count, step):
    if count <= 16:
        for i in range(count):
            step(i)
    else:
        lax.fori_loop(0, count, lambda i, c: (step(i), c)[1], 0)


def kernel(
    nr, ns, nc, lengths,
    acts_hbm, grads_hbm, pin_hbm, pout_hbm, bin_hbm, bout_hbm, eig_hbm, store_hbm, cand_hbm,
    scores_ref, picked_ref,
    acts, grads, pin, pout, bin_, bout, eig, store, cand,
    storef, tsend, trecv, total, precv, srecv, ssend,
    load_sem, small_sem, ts_sem, tr_sem, ps_sem, pr_sem, ss_sem, sr_sem, xs_sem, xr_sem,
):
    nl, tok, width = acts.shape
    rank = pin.shape[1]
    rdev = store.shape[1]
    half = rank // 2
    wide = 2 * rank
    nx = nr // nc
    n, nf = nr * ns, nx * ns
    row, seq = lax.axis_index("rows"), lax.axis_index("seq")
    mx, mc = row // nc, lax.rem(row, nc)
    me, mf = row * ns + seq, mx * ns + seq

    groups = []
    for l in range(nl):
        copies = (
            (pin_hbm.at[l], pin.at[l]), (pout_hbm.at[l], pout.at[l]),
            (acts_hbm.at[l, 0], acts.at[l]), (grads_hbm.at[l, 0], grads.at[l]),
        )
        groups.append([pltpu.make_async_copy(src, dst, load_sem.at[l, i]) for i, (src, dst) in enumerate(copies)])
    small = [
        pltpu.make_async_copy(src, dst, small_sem.at[i])
        for i, (src, dst) in enumerate((
            (bin_hbm, bin_), (bout_hbm, bout), (eig_hbm, eig), (cand_hbm, cand), (store_hbm, store.at[mc]),
        ))
    ]

    barrier = pltpu.get_barrier_semaphore()

    few = n <= 16
    away = [(k, x, c) for k in range(ns) for x in reversed(range(nx)) for c in range(nc)]

    def place(k, x, c):
        to = seq if k == ns - 1 else farther(seq, ns, k)
        return {"rows": lax.rem(mx + x, nx) * nc + lax.rem(mc + c, nc), "seq": to}

    def peer(e):
        if few:
            return place(*[m for m in away if m != (ns - 1, 0, 0)][e])
        to = lax.rem(me + e + 1, n)
        return {"rows": to // ns, "seq": lax.rem(to, ns)}

    def friend(e):
        if few:
            return place(*[m for m in away if m[2] == 0 and m != (ns - 1, 0, 0)][e])
        to = lax.rem(mf + e + 1, nf)
        return {"rows": to // ns * nc + mc, "seq": lax.rem(to, ns)}

    def sibling(e):
        return {"rows": mx * nc + lax.rem(mc + e + 1, nc)}

    for c in small[:3]:
        c.start()
    for c in groups[0]:
        c.start()
    each(n - 1, lambda e: pl.semaphore_signal(barrier, inc=1, device_id=peer(e), device_id_type=MESH))
    for g in groups[1:]:
        for c in g:
            c.start()
    for c in small[3:]:
        c.start()
    for c in small[:3]:
        c.wait()
    i0 = lax.broadcasted_iota(jnp.int32, (rank, rank), 0)
    i1 = lax.broadcasted_iota(jnp.int32, (rank, rank), 1)
    order = (i1 == jnp.where(i0 < half, 2 * i0, 2 * (i0 - half) + 1)).astype(BF16)
    w_in, w_out, w_rot, w_back, inv = [], [], [], [], []
    for l in range(nl):
        hi, lo = split(bin_[l])
        w = stack(hi, lo)
        w_in.append(lanes(w, w))
        hi, lo = split(jnp.transpose(bin_[l]))
        w = stack(hi, hi, lo, jnp.zeros_like(lo))
        w_rot.append(lanes(w, w))
        hi, lo = split(jnp.transpose(bout[l]))
        w_out.append(lanes(hi, lo))
        hi, lo = (mm(order, x).astype(BF16) for x in split(bout[l]))
        w_back.append(lanes(hi, hi, lo))
        v = 1.0 / (eig[l] + damping)
        inv.append(lanes(v, v))

    pos = seq * tok + lax.broadcasted_iota(jnp.int32, (tok, rank), 0)
    keep = pos < lengths[0]
    low = lax.broadcasted_iota(jnp.int32, (rank, wide), 1) < rank
    pa, pgt = [None] * nl, [None] * nl
    for l in range(nl):
        for c in groups[l]:
            c.wait()
        pa[l] = mm(acts[l], pin[l], NT)
        pgt[l] = mm(pout[l], grads[l], NT)
    ls = range(nl)
    pa = [jnp.where(keep, x.astype(BF16).astype(F32), 0.0).astype(BF16) for x in pa]
    pgt = [x.astype(BF16) for x in pgt]
    u = [split(mm(lanes(pa[l], pa[l]), w_in[l])) for l in ls]
    v = [split(mm(w_out[l], stack(pgt[l], pgt[l]))) for l in ls]
    rot = [mm(lanes(v[l][0], v[l][1], v[l][0]), stack(u[l][0], u[l][0], u[l][1])) for l in ls]
    pre = [split(rot[l] * inv[l]) for l in ls]
    x2 = [split(mm(lanes(jnp.where(low, *pre[l]), pre[l][0]), w_rot[l])) for l in ls]
    z = [mm(w_back[l], stack(x2[l][0], x2[l][1], x2[l][0])) for l in ls]
    for l in ls:
        tsend[pl.ds(l * half, half), :] = jnp.where(low[:half], z[l][:half], z[l][half:]).astype(BF16)

    pl.semaphore_wait(barrier, n - 1)

    def tcopy(e):
        return pltpu.make_async_remote_copy(
            src_ref=tsend, dst_ref=trecv.at[mf], send_sem=ts_sem.at[0], recv_sem=tr_sem.at[0],
            device_id=friend(e), device_id_type=MESH)

    def xcopy(e):
        return pltpu.make_async_remote_copy(
            src_ref=store.at[mc], dst_ref=store.at[mc], send_sem=xs_sem.at[e], recv_sem=xr_sem.at[e],
            device_id=sibling(e), device_id_type=MESH)

    each(nf - 1, lambda e: tcopy(e).start())
    for c in small[3:]:
        c.wait()
    each(nc - 1, lambda e: xcopy(e).start())
    trecv[pl.ds(mf, 1)] = tsend[...][None]

    rows = nc * rdev
    eye = lax.broadcasted_iota(jnp.int32, (rows, rdev), 0)
    col_of = lax.broadcasted_iota(jnp.int32, (rows, rdev), 1)
    r = lax.broadcasted_iota(jnp.int32, (rows, cand.shape[1]), 0)
    rows_k = ((mx * nc + r // rdev) * ns + seq) * rdev + lax.rem(r, rdev)

    hits = [cand[pl.ds(x * nc + mc, 1), :] == rows_k for x in range(nx)]
    each(nc - 1, lambda e: xcopy(e).wait_recv())
    for c in range(nl * half):
        at = slice(c * wide, (c + 1) * wide)
        storef[:, at] = store[:, :, at].astype(F32).reshape(rows, wide)
    others = trecv.at[pl.ds(0, nf - 1)]
    pltpu.make_async_copy(others, others, tr_sem.at[0]).wait()
    for x in range(nx):
        t = trecv[x * ns].astype(F32)
        for s in range(1, ns):
            t = t + trecv[x * ns + s].astype(F32)
        total[x] = t
    acc = [jnp.zeros((rows, wide), F32) for _ in range(nx)]
    for c in range(nl * half):
        s = storef[:, c * wide:(c + 1) * wide]
        for x in range(nx):
            acc[x] = acc[x] + s * total[x, c:c + 1, :]
    cols = [jnp.sum(a, axis=1, keepdims=True) for a in acc]
    for x in range(nx):
        precv[pl.ds(me, 1), x:x + 1, :] = jnp.sum(jnp.where(hits[x], cols[x], 0.0), axis=0, keepdims=True)[None]

    def pcopy(e):
        return pltpu.make_async_remote_copy(
            src_ref=precv.at[me], dst_ref=precv.at[me], send_sem=ps_sem.at[0], recv_sem=pr_sem.at[0],
            device_id=peer(e), device_id_type=MESH)

    each(n - 1, lambda e: pcopy(e).start())

    for x in range(nx):
        for c in range(nc):
            ssend[c, x:x + 1, :] = jnp.sum(
                jnp.where(eye == col_of + c * rdev, cols[x], 0.0), axis=0, keepdims=True)

    def scopy(e):
        return pltpu.make_async_remote_copy(
            src_ref=ssend.at[lax.rem(mc + e + 1, nc)], dst_ref=srecv.at[mc],
            send_sem=ss_sem.at[e], recv_sem=sr_sem.at[e],
            device_id=sibling(e), device_id_type=MESH)

    each(nc - 1, lambda e: scopy(e).start())
    srecv[pl.ds(mc, 1)] = ssend[pl.ds(mc, 1)]
    each(nc - 1, lambda e: scopy(e).wait_recv())
    for x in range(nx):
        for c in range(nc):
            scores_ref[x * nc + c:x * nc + c + 1, :] = srecv[c, x:x + 1, :]
    each(nc - 1, lambda e: scopy(e).wait_send())
    each(nc - 1, lambda e: xcopy(e).wait_send())
    pltpu.make_async_copy(others, others, ts_sem.at[0]).wait()

    others = precv.at[pl.ds(0, n - 1)]
    pltpu.make_async_copy(others, others, pr_sem.at[0]).wait()
    for c in range(nc):
        p = None
        for x in range(nx):
            at = (x * nc + c) * ns
            q = jnp.sum(precv[at:at + ns], axis=0)
            p = q if p is None else p + q
        for x in range(nx):
            picked_ref[x * nc + c:x * nc + c + 1, :] = p[x:x + 1, :]
    pltpu.make_async_copy(others, others, ps_sem.at[0]).wait()


def body(nr, ns, activations, out_grads, lengths, proj_in, proj_out,
         basis_in, basis_out, eigen, store, candidates):
    nl, _, tok, width = activations.shape
    rank = proj_in.shape[2]
    rdev, flat = store.shape
    batch, topk = candidates.shape
    nc = 2 if nr % 2 == 0 else 1
    nx = nr // nc
    n, nf = nr * ns, nx * ns
    dma = pltpu.SemaphoreType.DMA
    vm = pltpu.VMEM
    hbm = pl.BlockSpec(memory_space=pltpu.HBM)
    scores, picked = pl.pallas_call(
        functools.partial(kernel, nr, ns, nc),
        out_shape=(pltpu.VMEM((batch, rdev), F32), pltpu.VMEM((batch, topk), F32)),
        in_specs=[pl.BlockSpec(memory_space=pltpu.SMEM)] + [hbm] * 9,
        out_specs=(pl.BlockSpec(memory_space=pltpu.VMEM),) * 2,
        scratch_shapes=[
            vm((nl, tok, width), BF16), vm((nl, tok, width), BF16),
            vm((nl, rank, width), BF16), vm((nl, rank, width), BF16),
            vm((nl, rank, rank), F32), vm((nl, rank, rank), F32), vm((nl, rank, rank), F32),
            vm((nc, rdev, flat), BF16), vm((batch, topk), jnp.int32),
            vm((nc * rdev, flat), F32),
            vm((nl * rank // 2, 2 * rank), BF16), vm((nf, nl * rank // 2, 2 * rank), BF16),
            vm((nx, nl * rank // 2, 2 * rank), F32),
            vm((n, nx, topk), F32), vm((nc, nx, rdev), F32), vm((nc, nx, rdev), F32),
            dma((nl, 4)), dma((5,)),
            dma((1,)), dma((1,)), dma((1,)), dma((1,)),
            dma((nc,)), dma((nc,)), dma((nc,)), dma((nc,)),
        ],
        compiler_params=pltpu.CompilerParams(
            collective_id=0, has_side_effects=True, vmem_limit_bytes=60 * 2**20),
    )(
        lengths, activations, out_grads,
        jnp.swapaxes(proj_in, 1, 2), jnp.swapaxes(proj_out, 1, 2),
        basis_in, basis_out, eigen, store, candidates,
    )
    return scores.T, picked


def solution(mesh):
    placed = (
        P(None, ("groups", "rows"), "seq", None),
        P(None, ("groups", "rows"), "seq", None),
        P(("groups", "rows")),
        P(),
        P(),
        P(),
        P(),
        P(),
        P(("groups", "rows", "seq"), None),
        P("groups", None),
    )
    return jax.shard_map(
        functools.partial(body, mesh.shape["rows"], mesh.shape["seq"]),
        mesh=mesh,
        in_specs=placed,
        out_specs=(P(("groups", "rows", "seq"), None), P("groups", None)),
        check_vma=False,
    )
```

```python
import functools

import jax
import jax.numpy as jnp
from jax import lax
from jax.experimental import pallas as pl
from jax.experimental.pallas import tpu as pltpu
from jax.sharding import PartitionSpec as P

damping = 1.0
MESH = pl.DeviceIdType.MESH
F32 = jnp.float32
BF16 = jnp.bfloat16
NN = (((1,), (0,)), ((), ()))
NT = (((1,), (1,)), ((), ()))


def mm(a, b, dims=NN):
    return lax.dot_general(a, b, dims, preferred_element_type=F32)


def split(x):
    hi = x.astype(BF16)
    return hi, (x - hi.astype(F32)).astype(BF16)


def lanes(*parts):
    return jnp.concatenate(parts, axis=1)


def stack(*parts):
    return jnp.concatenate(parts, axis=0)


def farther(i, size, k):
    end = 2 * i // size
    near = i + end * (size - 1 - 2 * i)
    at = size - 1 - k
    at = at - (near - at + size) // size
    return at + end * (size - 1 - 2 * at)


def each(count, step):
    if count <= 16:
        for i in range(count):
            step(i)
    else:
        lax.fori_loop(0, count, lambda i, c: (step(i), c)[1], 0)


def kernel(
    nr, ns, nc, lengths,
    acts_hbm, grads_hbm, pin_hbm, pout_hbm, bin_hbm, bout_hbm, eig_hbm, store_hbm, cand_hbm,
    scores_ref, picked_ref,
    acts, grads, pin, pout, bin_, bout, eig, store, cand,
    storef, tsend, trecv, total, precv, srecv, ssend,
    load_sem, small_sem, ts_sem, tr_sem, ps_sem, pr_sem, ss_sem, sr_sem, xs_sem, xr_sem,
):
    nl, tok, width = acts.shape
    rank = pin.shape[1]
    rdev = store.shape[1]
    half = rank // 2
    wide = 2 * rank
    nx = nr // nc
    n, nf = nr * ns, nx * ns
    row, seq = lax.axis_index("rows"), lax.axis_index("seq")
    mx, mc = row // nc, lax.rem(row, nc)
    me, mf = row * ns + seq, mx * ns + seq

    groups = []
    for l in range(nl):
        copies = (
            (pin_hbm.at[l], pin.at[l]), (acts_hbm.at[l, 0], acts.at[l]),
            (pout_hbm.at[l], pout.at[l]), (grads_hbm.at[l, 0], grads.at[l]),
        )
        groups.append([pltpu.make_async_copy(src, dst, load_sem.at[l, i]) for i, (src, dst) in enumerate(copies)])
    small = [
        pltpu.make_async_copy(src, dst, small_sem.at[i])
        for i, (src, dst) in enumerate((
            (bin_hbm, bin_), (bout_hbm, bout), (eig_hbm, eig), (cand_hbm, cand), (store_hbm, store.at[mc]),
        ))
    ]

    barrier = pltpu.get_barrier_semaphore()

    few = n <= 16
    away = [(k, x, c) for k in range(ns) for x in reversed(range(nx)) for c in range(nc)]

    def place(k, x, c):
        to = seq if k == ns - 1 else farther(seq, ns, k)
        return {"rows": lax.rem(mx + x, nx) * nc + lax.rem(mc + c, nc), "seq": to}

    def peer(e):
        if few:
            return place(*[m for m in away if m != (ns - 1, 0, 0)][e])
        to = lax.rem(me + e + 1, n)
        return {"rows": to // ns, "seq": lax.rem(to, ns)}

    def friend(e):
        if few:
            return place(*[m for m in away if m[2] == 0 and m != (ns - 1, 0, 0)][e])
        to = lax.rem(mf + e + 1, nf)
        return {"rows": to // ns * nc + mc, "seq": lax.rem(to, ns)}

    def sibling(e):
        return {"rows": mx * nc + lax.rem(mc + e + 1, nc)}

    for c in small[:3]:
        c.start()
    for c in groups[0]:
        c.start()
    each(n - 1, lambda e: pl.semaphore_signal(barrier, inc=1, device_id=peer(e), device_id_type=MESH))
    for g in groups[1:]:
        for c in g:
            c.start()
    for c in small[3:]:
        c.start()
    for c in small[:3]:
        c.wait()
    i0 = lax.broadcasted_iota(jnp.int32, (rank, rank), 0)
    i1 = lax.broadcasted_iota(jnp.int32, (rank, rank), 1)
    order = (i1 == jnp.where(i0 < half, 2 * i0, 2 * (i0 - half) + 1)).astype(BF16)
    w_in, w_out, w_rot, w_back, inv = [], [], [], [], []
    for l in range(nl):
        hi, lo = split(bin_[l])
        w = stack(hi, lo)
        w_in.append(lanes(w, w))
        hi, lo = split(jnp.transpose(bin_[l]))
        w = stack(hi, hi, lo, jnp.zeros_like(lo))
        w_rot.append(lanes(w, w))
        hi, lo = split(jnp.transpose(bout[l]))
        w_out.append(lanes(hi, lo))
        hi, lo = (mm(order, x).astype(BF16) for x in split(bout[l]))
        w_back.append(lanes(hi, hi, lo))
        v = 1.0 / (eig[l] + damping)
        inv.append(lanes(v, v))

    pos = seq * tok + lax.broadcasted_iota(jnp.int32, (tok, rank), 0)
    keep = pos < lengths[0]
    low = lax.broadcasted_iota(jnp.int32, (rank, wide), 1) < rank
    pa, pgt = [None] * nl, [None] * nl
    for l in range(nl):
        for c in groups[l]:
            c.wait()
        pa[l] = mm(acts[l], pin[l], NT)
        pgt[l] = mm(pout[l], grads[l], NT)
    ls = range(nl)
    pa = [jnp.where(keep, x.astype(BF16).astype(F32), 0.0).astype(BF16) for x in pa]
    pgt = [x.astype(BF16) for x in pgt]
    u = [split(mm(pa[l], w_in[l][:rank]) + mm(pa[l], w_in[l][rank:])) for l in ls]
    v = [split(mm(w_out[l], stack(pgt[l], pgt[l]))) for l in ls]
    rot = [mm(lanes(v[l][0], v[l][1], v[l][0]), stack(u[l][0], u[l][0], u[l][1])) for l in ls]
    pre = [split(rot[l] * inv[l]) for l in ls]
    x2 = [split(mm(lanes(jnp.where(low, *pre[l]), pre[l][0]), w_rot[l])) for l in ls]
    z = [mm(w_back[l], stack(x2[l][0], x2[l][1], x2[l][0])) for l in ls]
    for l in ls:
        tsend[pl.ds(l * half, half), :] = jnp.where(low[:half], z[l][:half], z[l][half:]).astype(BF16)

    pl.semaphore_wait(barrier, n - 1)

    def tcopy(e):
        return pltpu.make_async_remote_copy(
            src_ref=tsend, dst_ref=trecv.at[mf], send_sem=ts_sem.at[0], recv_sem=tr_sem.at[mx],
            device_id=friend(e), device_id_type=MESH)

    def xcopy(e):
        return pltpu.make_async_remote_copy(
            src_ref=store.at[mc], dst_ref=store.at[mc], send_sem=xs_sem.at[e], recv_sem=xr_sem.at[e],
            device_id=sibling(e), device_id_type=MESH)

    each(nf - 1, lambda e: tcopy(e).start())
    for c in small[3:]:
        c.wait()
    each(nc - 1, lambda e: xcopy(e).start())
    trecv[pl.ds(mf, 1)] = tsend[...][None]

    rows = nc * rdev
    eye = lax.broadcasted_iota(jnp.int32, (rows, rdev), 0)
    col_of = lax.broadcasted_iota(jnp.int32, (rows, rdev), 1)
    r = lax.broadcasted_iota(jnp.int32, (rows, cand.shape[1]), 0)
    rows_k = ((mx * nc + r // rdev) * ns + seq) * rdev + lax.rem(r, rdev)

    each(nc - 1, lambda e: xcopy(e).wait_recv())
    for c in range(nl * half):
        at = slice(c * wide, (c + 1) * wide)
        storef[:, at] = store[:, :, at].astype(F32).reshape(rows, wide)

    cols = []
    for x in range(nx):
        hit = cand[pl.ds(x * nc + mc, 1), :] == rows_k
        for own in range(2):
            @pl.when((mx == x) if own else (mx != x))
            def _():
                if ns > own:
                    came = trecv.at[pl.ds(0, ns - own)]
                    pltpu.make_async_copy(came, came, tr_sem.at[x]).wait()

        t = trecv[x * ns].astype(F32)
        for z in range(1, ns):
            t = t + trecv[x * ns + z].astype(F32)
        total[x] = t
        acc = [jnp.zeros((rows, wide), F32) for _ in range(2)]
        for c in range(nl * half):
            acc[c % 2] = acc[c % 2] + storef[:, c * wide:(c + 1) * wide] * total[x, c:c + 1, :]
        cols.append(jnp.sum(acc[0] + acc[1], axis=1, keepdims=True))
        precv[pl.ds(me, 1), x:x + 1, :] = jnp.sum(jnp.where(hit, cols[x], 0.0), axis=0, keepdims=True)[None]

    def pcopy(e):
        return pltpu.make_async_remote_copy(
            src_ref=precv.at[me], dst_ref=precv.at[me], send_sem=ps_sem.at[0], recv_sem=pr_sem.at[0],
            device_id=peer(e), device_id_type=MESH)

    each(n - 1, lambda e: pcopy(e).start())

    for x in range(nx):
        for c in range(nc):
            ssend[c, x:x + 1, :] = jnp.sum(
                jnp.where(eye == col_of + c * rdev, cols[x], 0.0), axis=0, keepdims=True)

    def scopy(e):
        return pltpu.make_async_remote_copy(
            src_ref=ssend.at[lax.rem(mc + e + 1, nc)], dst_ref=srecv.at[mc],
            send_sem=ss_sem.at[e], recv_sem=sr_sem.at[e],
            device_id=sibling(e), device_id_type=MESH)

    each(nc - 1, lambda e: scopy(e).start())
    srecv[pl.ds(mc, 1)] = ssend[pl.ds(mc, 1)]
    each(nc - 1, lambda e: scopy(e).wait_recv())
    for x in range(nx):
        for c in range(nc):
            scores_ref[x * nc + c:x * nc + c + 1, :] = srecv[c, x:x + 1, :]
    each(nc - 1, lambda e: scopy(e).wait_send())
    each(nc - 1, lambda e: xcopy(e).wait_send())
    sent = trecv.at[pl.ds(0, nf - 1)]
    pltpu.make_async_copy(sent, sent, ts_sem.at[0]).wait()

    others = precv.at[pl.ds(0, n - 1)]
    pltpu.make_async_copy(others, others, pr_sem.at[0]).wait()
    for c in range(nc):
        p = None
        for x in range(nx):
            at = (x * nc + c) * ns
            q = jnp.sum(precv[at:at + ns], axis=0)
            p = q if p is None else p + q
        for x in range(nx):
            picked_ref[x * nc + c:x * nc + c + 1, :] = p[x:x + 1, :]
    pltpu.make_async_copy(others, others, ps_sem.at[0]).wait()


def body(nr, ns, activations, out_grads, lengths, proj_in, proj_out,
         basis_in, basis_out, eigen, store, candidates):
    nl, _, tok, width = activations.shape
    rank = proj_in.shape[2]
    rdev, flat = store.shape
    batch, topk = candidates.shape
    nc = 2 if nr % 2 == 0 else 1
    nx = nr // nc
    n, nf = nr * ns, nx * ns
    dma = pltpu.SemaphoreType.DMA
    vm = pltpu.VMEM
    hbm = pl.BlockSpec(memory_space=pltpu.HBM)
    scores, picked = pl.pallas_call(
        functools.partial(kernel, nr, ns, nc),
        out_shape=(pltpu.VMEM((batch, rdev), F32), pltpu.VMEM((batch, topk), F32)),
        in_specs=[pl.BlockSpec(memory_space=pltpu.SMEM)] + [hbm] * 9,
        out_specs=(pl.BlockSpec(memory_space=pltpu.VMEM),) * 2,
        scratch_shapes=[
            vm((nl, tok, width), BF16), vm((nl, tok, width), BF16),
            vm((nl, rank, width), BF16), vm((nl, rank, width), BF16),
            vm((nl, rank, rank), F32), vm((nl, rank, rank), F32), vm((nl, rank, rank), F32),
            vm((nc, rdev, flat), BF16), vm((batch, topk), jnp.int32),
            vm((nc * rdev, flat), F32),
            vm((nl * rank // 2, 2 * rank), BF16), vm((nf, nl * rank // 2, 2 * rank), BF16),
            vm((nx, nl * rank // 2, 2 * rank), F32),
            vm((n, nx, topk), F32), vm((nc, nx, rdev), F32), vm((nc, nx, rdev), F32),
            dma((nl, 4)), dma((5,)),
            dma((1,)), dma((nx,)), dma((1,)), dma((1,)),
            dma((nc,)), dma((nc,)), dma((nc,)), dma((nc,)),
        ],
        compiler_params=pltpu.CompilerParams(
            collective_id=0, has_side_effects=True, vmem_limit_bytes=60 * 2**20),
    )(
        lengths, activations, out_grads,
        jnp.swapaxes(proj_in, 1, 2), jnp.swapaxes(proj_out, 1, 2),
        basis_in, basis_out, eigen, store, candidates,
    )
    return scores.T, picked


def solution(mesh):
    placed = (
        P(None, ("groups", "rows"), "seq", None),
        P(None, ("groups", "rows"), "seq", None),
        P(("groups", "rows")),
        P(),
        P(),
        P(),
        P(),
        P(),
        P(("groups", "rows", "seq"), None),
        P("groups", None),
    )
    return jax.shard_map(
        functools.partial(body, mesh.shape["rows"], mesh.shape["seq"]),
        mesh=mesh,
        in_specs=placed,
        out_specs=(P(("groups", "rows", "seq"), None), P("groups", None)),
        check_vma=False,
    )
```

```python
import functools

import jax
import jax.numpy as jnp
from jax import lax
from jax.experimental import pallas as pl
from jax.experimental.pallas import tpu as pltpu
from jax.sharding import PartitionSpec as P

damping = 1.0
MESH = pl.DeviceIdType.MESH
F32 = jnp.float32
BF16 = jnp.bfloat16
NN = (((1,), (0,)), ((), ()))
NT = (((1,), (1,)), ((), ()))


def mm(a, b, dims=NN):
    return lax.dot_general(a, b, dims, preferred_element_type=F32)


def split(x):
    hi = x.astype(BF16)
    return hi, (x - hi.astype(F32)).astype(BF16)


def lanes(*parts):
    return jnp.concatenate(parts, axis=1)


def stack(*parts):
    return jnp.concatenate(parts, axis=0)


def farther(i, size, k):
    end = 2 * i // size
    near = i + end * (size - 1 - 2 * i)
    at = size - 1 - k
    at = at - (near - at + size) // size
    return at + end * (size - 1 - 2 * at)


def each(count, step):
    if count <= 16:
        for i in range(count):
            step(i)
    else:
        lax.fori_loop(0, count, lambda i, c: (step(i), c)[1], 0)


def kernel(
    nr, ns, nc, lengths,
    acts_hbm, grads_hbm, pin_hbm, pout_hbm, bin_hbm, bout_hbm, eig_hbm, store_hbm, cand_hbm,
    scores_ref, picked_ref,
    acts, grads, pin, pout, bin_, bout, eig, store, cand,
    storef, tsend, trecv, precv, srecv, ssend,
    load_sem, small_sem, ts_sem, tr_sem, ps_sem, pr_sem, ss_sem, sr_sem, xs_sem, xr_sem,
):
    nl, tok, width = acts.shape
    rank = pin.shape[1]
    rdev = store.shape[1]
    half = rank // 2
    wide = 2 * rank
    nx = nr // nc
    n, nf = nr * ns, nx * ns
    row, seq = lax.axis_index("rows"), lax.axis_index("seq")
    mx, mc = row // nc, lax.rem(row, nc)
    me, mf = row * ns + seq, mx * ns + seq

    groups = []
    for l in range(nl):
        copies = (
            (pin_hbm.at[l], pin.at[l]), (acts_hbm.at[l, 0], acts.at[l]),
            (pout_hbm.at[l], pout.at[l]), (grads_hbm.at[l, 0], grads.at[l]),
        )
        groups.append([pltpu.make_async_copy(src, dst, load_sem.at[l, i]) for i, (src, dst) in enumerate(copies)])
    small = [
        pltpu.make_async_copy(src, dst, small_sem.at[i])
        for i, (src, dst) in enumerate((
            (bin_hbm, bin_), (bout_hbm, bout), (eig_hbm, eig), (cand_hbm, cand), (store_hbm, store.at[mc]),
        ))
    ]

    barrier = pltpu.get_barrier_semaphore()

    few = n <= 16
    away = [(k, x, c) for k in range(ns) for x in reversed(range(nx)) for c in range(nc)]

    def place(k, x, c):
        to = seq if k == ns - 1 else farther(seq, ns, k)
        return {"rows": lax.rem(mx + x, nx) * nc + lax.rem(mc + c, nc), "seq": to}

    def peer(e):
        if few:
            return place(*[m for m in away if m != (ns - 1, 0, 0)][e])
        to = lax.rem(me + e + 1, n)
        return {"rows": to // ns, "seq": lax.rem(to, ns)}

    def friend(e):
        if few:
            return place(*[m for m in away if m[2] == 0 and m != (ns - 1, 0, 0)][e])
        to = lax.rem(mf + e + 1, nf)
        return {"rows": to // ns * nc + mc, "seq": lax.rem(to, ns)}

    def sibling(e):
        return {"rows": mx * nc + lax.rem(mc + e + 1, nc)}

    for c in small[:3]:
        c.start()
    for c in groups[0]:
        c.start()
    each(n - 1, lambda e: pl.semaphore_signal(barrier, inc=1, device_id=peer(e), device_id_type=MESH))
    for g in groups[1:]:
        for c in g:
            c.start()
    for c in small[3:]:
        c.start()
    for c in small[:3]:
        c.wait()
    i0 = lax.broadcasted_iota(jnp.int32, (rank, rank), 0)
    i1 = lax.broadcasted_iota(jnp.int32, (rank, rank), 1)
    order = (i1 == jnp.where(i0 < half, 2 * i0, 2 * (i0 - half) + 1)).astype(BF16)
    w_in, w_out, w_rot, w_back, inv = [], [], [], [], []
    for l in range(nl):
        hi, lo = split(bin_[l])
        w = stack(hi, lo)
        w_in.append(lanes(w, w))
        hi, lo = split(jnp.transpose(bin_[l]))
        w = stack(hi, hi, lo, jnp.zeros_like(lo))
        w_rot.append(lanes(w, w))
        hi, lo = split(jnp.transpose(bout[l]))
        w_out.append(lanes(hi, lo))
        hi, lo = (mm(order, x).astype(BF16) for x in split(bout[l]))
        w_back.append(lanes(hi, hi, lo))
        v = 1.0 / (eig[l] + damping)
        inv.append(lanes(v, v))

    pos = seq * tok + lax.broadcasted_iota(jnp.int32, (tok, rank), 0)
    keep = pos < lengths[0]
    low = lax.broadcasted_iota(jnp.int32, (rank, wide), 1) < rank
    pa, pgt = [None] * nl, [None] * nl
    for l in range(nl):
        for c in groups[l]:
            c.wait()
        pa[l] = mm(acts[l], pin[l], NT)
        pgt[l] = mm(pout[l], grads[l], NT)
    ls = range(nl)
    pa = [jnp.where(keep, x.astype(BF16).astype(F32), 0.0).astype(BF16) for x in pa]
    pgt = [x.astype(BF16) for x in pgt]
    u = [split(mm(pa[l], w_in[l][:rank]) + mm(pa[l], w_in[l][rank:])) for l in ls]
    v = [split(mm(w_out[l], stack(pgt[l], pgt[l]))) for l in ls]
    rot = [mm(lanes(v[l][0], v[l][1], v[l][0]), stack(u[l][0], u[l][0], u[l][1])) for l in ls]
    pre = [split(rot[l] * inv[l]) for l in ls]
    x2 = [split(mm(lanes(jnp.where(low, *pre[l]), pre[l][0]), w_rot[l])) for l in ls]
    z = [mm(w_back[l], stack(x2[l][0], x2[l][1], x2[l][0])) for l in ls]
    for l in ls:
        tsend[pl.ds(l * half, half), :] = jnp.where(low[:half], z[l][:half], z[l][half:]).astype(BF16)

    pl.semaphore_wait(barrier, n - 1)

    def tcopy(e):
        return pltpu.make_async_remote_copy(
            src_ref=tsend, dst_ref=trecv.at[mf], send_sem=ts_sem.at[0], recv_sem=tr_sem.at[mx],
            device_id=friend(e), device_id_type=MESH)

    def xcopy(e):
        return pltpu.make_async_remote_copy(
            src_ref=store.at[mc], dst_ref=store.at[mc], send_sem=xs_sem.at[e], recv_sem=xr_sem.at[e],
            device_id=sibling(e), device_id_type=MESH)

    each(nf - 1, lambda e: tcopy(e).start())
    for c in small[3:]:
        c.wait()
    each(nc - 1, lambda e: xcopy(e).start())
    trecv[pl.ds(mf, 1)] = tsend[...][None]

    rows = nc * rdev
    eye = lax.broadcasted_iota(jnp.int32, (rows, rdev), 0)
    col_of = lax.broadcasted_iota(jnp.int32, (rows, rdev), 1)
    r = lax.broadcasted_iota(jnp.int32, (rows, cand.shape[1]), 0)
    rows_k = ((mx * nc + r // rdev) * ns + seq) * rdev + lax.rem(r, rdev)

    each(nc - 1, lambda e: xcopy(e).wait_recv())
    for c in range(nl * half):
        at = slice(c * wide, (c + 1) * wide)
        storef[:, at] = store[:, :, at].astype(F32).reshape(rows, wide)

    cols = []
    for x in range(nx):
        hit = cand[pl.ds(x * nc + mc, 1), :] == rows_k
        for own in range(2):
            @pl.when((mx == x) if own else (mx != x))
            def _():
                if ns > own:
                    came = trecv.at[pl.ds(0, ns - own)]
                    pltpu.make_async_copy(came, came, tr_sem.at[x]).wait()

        t = trecv[x * ns].astype(F32)
        for z in range(1, ns):
            t = t + trecv[x * ns + z].astype(F32)
        acc = [jnp.zeros((rows, wide), F32) for _ in range(2)]
        for c in range(nl * half):
            acc[c % 2] = acc[c % 2] + storef[:, c * wide:(c + 1) * wide] * t[c:c + 1, :]
        cols.append(jnp.sum(acc[0] + acc[1], axis=1, keepdims=True))
        precv[pl.ds(me, 1), x:x + 1, :] = jnp.sum(jnp.where(hit, cols[x], 0.0), axis=0, keepdims=True)[None]

    def pcopy(e):
        return pltpu.make_async_remote_copy(
            src_ref=precv.at[me], dst_ref=precv.at[me], send_sem=ps_sem.at[0], recv_sem=pr_sem.at[0],
            device_id=peer(e), device_id_type=MESH)

    each(n - 1, lambda e: pcopy(e).start())

    for x in range(nx):
        for c in range(nc):
            ssend[c, x:x + 1, :] = jnp.sum(
                jnp.where(eye == col_of + c * rdev, cols[x], 0.0), axis=0, keepdims=True)

    def scopy(e):
        return pltpu.make_async_remote_copy(
            src_ref=ssend.at[lax.rem(mc + e + 1, nc)], dst_ref=srecv.at[mc],
            send_sem=ss_sem.at[e], recv_sem=sr_sem.at[e],
            device_id=sibling(e), device_id_type=MESH)

    each(nc - 1, lambda e: scopy(e).start())
    srecv[pl.ds(mc, 1)] = ssend[pl.ds(mc, 1)]
    each(nc - 1, lambda e: scopy(e).wait_recv())
    for x in range(nx):
        for c in range(nc):
            scores_ref[x * nc + c:x * nc + c + 1, :] = srecv[c, x:x + 1, :]
    each(nc - 1, lambda e: scopy(e).wait_send())
    each(nc - 1, lambda e: xcopy(e).wait_send())
    sent = trecv.at[pl.ds(0, nf - 1)]
    pltpu.make_async_copy(sent, sent, ts_sem.at[0]).wait()

    others = precv.at[pl.ds(0, n - 1)]
    pltpu.make_async_copy(others, others, pr_sem.at[0]).wait()
    for c in range(nc):
        p = None
        for x in range(nx):
            at = (x * nc + c) * ns
            q = jnp.sum(precv[at:at + ns], axis=0)
            p = q if p is None else p + q
        for x in range(nx):
            picked_ref[x * nc + c:x * nc + c + 1, :] = p[x:x + 1, :]
    pltpu.make_async_copy(others, others, ps_sem.at[0]).wait()


def body(nr, ns, activations, out_grads, lengths, proj_in, proj_out,
         basis_in, basis_out, eigen, store, candidates):
    nl, _, tok, width = activations.shape
    rank = proj_in.shape[2]
    rdev, flat = store.shape
    batch, topk = candidates.shape
    nc = 2 if nr % 2 == 0 else 1
    nx = nr // nc
    n, nf = nr * ns, nx * ns
    dma = pltpu.SemaphoreType.DMA
    vm = pltpu.VMEM
    hbm = pl.BlockSpec(memory_space=pltpu.HBM)
    scores, picked = pl.pallas_call(
        functools.partial(kernel, nr, ns, nc),
        out_shape=(pltpu.VMEM((batch, rdev), F32), pltpu.VMEM((batch, topk), F32)),
        in_specs=[pl.BlockSpec(memory_space=pltpu.SMEM)] + [hbm] * 9,
        out_specs=(pl.BlockSpec(memory_space=pltpu.VMEM),) * 2,
        scratch_shapes=[
            vm((nl, tok, width), BF16), vm((nl, tok, width), BF16),
            vm((nl, rank, width), BF16), vm((nl, rank, width), BF16),
            vm((nl, rank, rank), F32), vm((nl, rank, rank), F32), vm((nl, rank, rank), F32),
            vm((nc, rdev, flat), BF16), vm((batch, topk), jnp.int32),
            vm((nc * rdev, flat), F32),
            vm((nl * rank // 2, 2 * rank), BF16), vm((nf, nl * rank // 2, 2 * rank), BF16),
            vm((n, nx, topk), F32), vm((nc, nx, rdev), F32), vm((nc, nx, rdev), F32),
            dma((nl, 4)), dma((5,)),
            dma((1,)), dma((nx,)), dma((1,)), dma((1,)),
            dma((nc,)), dma((nc,)), dma((nc,)), dma((nc,)),
        ],
        compiler_params=pltpu.CompilerParams(
            collective_id=0, has_side_effects=True, vmem_limit_bytes=60 * 2**20),
    )(
        lengths, activations, out_grads,
        jnp.swapaxes(proj_in, 1, 2), jnp.swapaxes(proj_out, 1, 2),
        basis_in, basis_out, eigen, store, candidates,
    )
    return scores.T, picked


def solution(mesh):
    placed = (
        P(None, ("groups", "rows"), "seq", None),
        P(None, ("groups", "rows"), "seq", None),
        P(("groups", "rows")),
        P(),
        P(),
        P(),
        P(),
        P(),
        P(("groups", "rows", "seq"), None),
        P("groups", None),
    )
    return jax.shard_map(
        functools.partial(body, mesh.shape["rows"], mesh.shape["seq"]),
        mesh=mesh,
        in_specs=placed,
        out_specs=(P(("groups", "rows", "seq"), None), P("groups", None)),
        check_vma=False,
    )
```
